32 devices in a mesh: row: 8 (over z, y), col: 4 (over x, core).
Axes of the slice: x: 2, y: 2, z: 4, core: 2. Of those that a mesh axis runs over, the one named last changes fastest.
Arguments:
- momentum: float32 [8192, 16384], P('row', 'col'), may hold values from -6 to 6
- grads: bfloat16 [2, 8192, 16384], P(None, 'row', 'col'), may hold values from -400 to 400
- basis: float32 [16384, 256], P('col'), may hold values from -0.046875 to 0.046875
Outputs:
- change: bfloat16 [8192, 16384], P('row', 'col')
- state: float32 [8192, 16384], P('row', 'col')
The draws below stay inside these ranges and needn't reach their ends.
All inputs are finite; a program needn't handle non-finite values.
Results may differ from the reference program's by a relative error of at most 0.0035.
Values sent between devices are 32-bit elements; how exact they have to be, the bound alone decides.
A program may use at most 192 MiB of HBM per device.

```python
import jax
import jax.numpy as jnp
from jax import lax

ROWS = 8192
COLS = 16384
RANK = 256
STEPS = 2


def draw_grads(key, part):
    row_key = jax.random.fold_in(key, 11)
    col_key = jax.random.fold_in(key, 12)
    base_key = jax.random.fold_in(key, 13)
    row_scale = jnp.exp(jax.random.uniform(row_key, (1, ROWS, 1), jnp.float32, jnp.log(0.3), jnp.log(3.0)))
    col_scale = jnp.exp(jax.random.uniform(col_key, (1, 1, COLS), jnp.float32, jnp.log(0.3), jnp.log(3.0)))
    values = jax.random.normal(base_key, (STEPS, ROWS, COLS), jnp.float32) * row_scale * col_scale
    return jnp.clip(values, -400.0, 400.0).astype(jnp.bfloat16)


def shard_levels(key, dims, shards, least, high):
    gain = 1.0
    for dim, blocks in shards:
        draws = jax.random.uniform(jax.random.fold_in(jax.random.fold_in(key, 6), dim), (blocks,), jnp.float32, least / len(shards), high / len(shards))
        gain = gain * jnp.repeat(jnp.exp(draws), dims[dim] // blocks).reshape((-1,) + (1,) * (len(dims) - 1 - dim))
    return gain


def gaussian(stream_key, shape, deviation, limit, pieces=(), dtype=jnp.bfloat16):
    gain = shard_levels(stream_key, shape, pieces, -0.22, 0.18) if pieces else 1.0
    entries = jax.random.normal(stream_key, shape, jnp.float32) * deviation * gain
    return jnp.minimum(jnp.maximum(entries, -limit), limit).astype(dtype)


def setup_inputs(seed: int = 0) -> dict:
    arg_keys = jax.random.split(jax.random.key(seed), 4)
    return {
        "momentum": gaussian(arg_keys[0], (ROWS, COLS), 1.0, 6.0, ((0, 8), (1, 4)), jnp.float32),
        "grads": draw_grads(jax.random.fold_in(arg_keys[3], 71), 0),
        "basis": gaussian(arg_keys[2], (COLS, RANK), COLS ** -0.5, 0.046875, ((0, 4),), jnp.float32),
    }


keep_rate = 0.95
norm_eps = 1e-06

def reference(momentum, grads, basis):
    high = lax.Precision.HIGHEST
    factor = (ROWS * COLS / RANK) ** 0.5
    state = momentum
    right = basis
    change = jnp.zeros(momentum.shape, jnp.float32)
    for step in range(STEPS):
        buffer = state + grads[step].astype(jnp.float32)
        projected = jnp.dot(buffer.astype(jnp.float32), right.astype(jnp.float32), precision=high, preferred_element_type=jnp.float32)
        gram = jnp.dot(projected.T.astype(jnp.float32), projected.astype(jnp.float32), precision=high, preferred_element_type=jnp.float32)
        lower = jnp.linalg.cholesky(gram)
        ortho = jax.scipy.linalg.solve_triangular(lower, projected.T, lower=True).T
        raw = lax.dot_general(buffer.astype(jnp.float32), ortho.astype(jnp.float32), (((0,), (0,)), ((), ())), precision=high, preferred_element_type=jnp.float32)
        scale = lax.rsqrt(lax.optimization_barrier(jnp.sum(raw * raw, axis=0)) + norm_eps)
        right = raw * scale
        state = buffer - (1.0 - keep_rate) * jnp.dot(ortho.astype(jnp.float32), raw.T.astype(jnp.float32), precision=high, preferred_element_type=jnp.float32)
        change = change + factor * jnp.dot(ortho.astype(jnp.float32), right.T.astype(jnp.float32), precision=high, preferred_element_type=jnp.float32)
    return (change.astype(jnp.bfloat16), state)
```

```python
import functools

import jax
import jax.numpy as jnp
from jax import lax
from jax.experimental import pallas as pl
from jax.experimental.pallas import tpu as pltpu
from jax.sharding import PartitionSpec as P

keep_rate = 0.95
norm_eps = 1e-06
HIGH = lax.Precision.HIGH
HIGHEST = lax.Precision.HIGHEST


def matmul(a, b, dims, precision):
    return lax.dot_general(a, b, (dims, ((), ())), precision=precision, preferred_element_type=jnp.float32)


def reduce_kernel(axis, bits, count, *refs):
    inputs, outs, recvs, works = (refs[k * count : (k + 1) * count] for k in range(4))
    send_sem, recv_sem = refs[4 * count :]
    me = lax.axis_index(axis)
    halves = [lax.rem(me // (1 << b), 2) for b in bits]
    partners = [me + (1 - 2 * h) * (1 << b) for h, b in zip(halves, bits)]
    barrier = pltpu.get_barrier_semaphore()
    for p in partners:
        pl.semaphore_signal(barrier, inc=1, device_id={axis: p}, device_id_type=pl.DeviceIdType.MESH)
    pl.semaphore_wait(barrier, len(bits))

    starts = [[0] for _ in range(count)]
    for s in range(len(bits)):
        copies = []
        for i in range(count):
            size = inputs[i].shape[0] >> (s + 1)
            base = inputs[i].shape[0] - 2 * size
            source = inputs[i] if s == 0 else works[i]
            there = pl.multiple_of(starts[i][s] + (1 - halves[s]) * size, 8)
            copy = pltpu.make_async_remote_copy(
                src_ref=source.at[pl.ds(there, size)],
                dst_ref=recvs[i].at[pl.ds(base, size)],
                send_sem=send_sem.at[i, s],
                recv_sem=recv_sem.at[i, s],
                device_id={axis: partners[s]},
                device_id_type=pl.DeviceIdType.MESH,
            )
            copy.start()
            copies.append(copy)
        for i in range(count):
            size = inputs[i].shape[0] >> (s + 1)
            base = inputs[i].shape[0] - 2 * size
            source = inputs[i] if s == 0 else works[i]
            here = pl.multiple_of(starts[i][s] + halves[s] * size, 8)
            copies[i].wait()
            target = outs[i] if s == len(bits) - 1 else works[i]
            target[pl.ds(here, size), :] = source[pl.ds(here, size), :] + recvs[i][pl.ds(base, size), :]
            starts[i].append(here)
    for s in reversed(range(len(bits))):
        t = 2 * len(bits) - 1 - s
        copies = []
        for i in range(count):
            size = inputs[i].shape[0] >> (s + 1)
            mine = outs[i].at[pl.ds(starts[i][s + 1], size)]
            copy = pltpu.make_async_remote_copy(
                src_ref=mine,
                dst_ref=mine,
                send_sem=send_sem.at[i, t],
                recv_sem=recv_sem.at[i, t],
                device_id={axis: partners[s]},
                device_id_type=pl.DeviceIdType.MESH,
            )
            copy.start()
            copies.append(copy)
        for copy in copies:
            copy.wait()


def all_reduce(arrays, axis, size, collective_id):
    bits = list(range(size.bit_length() - 1))
    count = len(arrays)
    total = sum(a.size for a in arrays)
    vmem = pl.BlockSpec(memory_space=pltpu.VMEM)
    return pl.pallas_call(
        functools.partial(reduce_kernel, axis, bits, count),
        out_shape=[jax.ShapeDtypeStruct(a.shape, a.dtype) for a in arrays],
        in_specs=[vmem] * count,
        out_specs=[vmem] * count,
        scratch_shapes=[pltpu.VMEM(a.shape, a.dtype) for a in arrays * 2]
        + [pltpu.SemaphoreType.DMA((count, 2 * len(bits))), pltpu.SemaphoreType.DMA((count, 2 * len(bits)))],
        compiler_params=pltpu.CompilerParams(
            collective_id=collective_id, has_side_effects=True, vmem_limit_bytes=16 * 2**20
        ),
        cost_estimate=pl.CostEstimate(flops=total, bytes_accessed=40 * total, transcendentals=0),
    )(*arrays)


def shards(row_size, col_size, momentum, grads, basis):
    rank = basis.shape[1]
    factor = (momentum.shape[0] * row_size * momentum.shape[1] * col_size / rank) ** 0.5
    eye = jnp.eye(rank, dtype=jnp.float32)
    state = momentum
    right = basis
    scale = None
    squares = None
    lefts, rights = [], []
    steps = grads.shape[0]
    for step in range(steps):
        buffer = state + grads[step].astype(jnp.float32)
        partial_value = matmul(buffer, right, ((1,), (0,)), HIGH)
        if step == 0:
            (projected,) = all_reduce([partial_value], "col", col_size, 0)
        else:
            projected, squares = all_reduce([partial_value, squares], "col", col_size, 1)
            scale = lax.rsqrt(squares[:1] + norm_eps)
            projected = projected * scale
            rights.append(right * scale)
        product = lax.psum(matmul(buffer, projected, ((0,), (0,)), HIGH), "row")
        part = matmul(projected, projected, ((0,), (0,)), HIGHEST)
        (gram,) = all_reduce([part], "row", row_size, 2)
        lower = jnp.linalg.cholesky(gram)
        inverse = jax.scipy.linalg.solve_triangular(lower, eye, lower=True)
        ortho = matmul(projected, inverse, ((1,), (1,)), HIGHEST)
        raw = matmul(product, inverse, ((1,), (1,)), HIGHEST)
        lefts.append(ortho)
        squares = jnp.pad(jnp.sum(raw * raw, axis=0, keepdims=True), ((0, 8 * col_size - 1), (0, 0)))
        right = raw
        state = buffer - (1.0 - keep_rate) * matmul(
            ortho.astype(jnp.bfloat16), raw.astype(jnp.bfloat16), ((1,), (1,)), None
        )
    (squares,) = all_reduce([squares], "col", col_size, 3)
    rights.append(right * lax.rsqrt(squares[:1] + norm_eps))
    change = factor * matmul(jnp.concatenate(lefts, 1), jnp.concatenate(rights, 1), ((1,), (1,)), HIGH)
    return (change.astype(jnp.bfloat16), state)


def solution(mesh):
    return jax.shard_map(
        functools.partial(shards, mesh.shape["row"], mesh.shape["col"]),
        mesh=mesh,
        in_specs=(P("row", "col"), P(None, "row", "col"), P("col", None)),
        out_specs=(P("row", "col"), P("row", "col")),
        check_vma=False,
    )
```

```python
import functools

import jax
import jax.numpy as jnp
from jax import lax
from jax.experimental import pallas as pl
from jax.experimental.pallas import tpu as pltpu
from jax.sharding import PartitionSpec as P

keep_rate = 0.95
norm_eps = 1e-06
HIGH = lax.Precision.HIGH
HIGHEST = lax.Precision.HIGHEST


def matmul(a, b, dims, precision):
    return lax.dot_general(a, b, (dims, ((), ())), precision=precision, preferred_element_type=jnp.float32)


def reduce_kernel(axis, orders, count, *refs):
    bits = range(len(orders[0]))
    inputs, outs, recvs, works = (refs[k * count : (k + 1) * count] for k in range(4))
    send_sem, recv_sem = refs[4 * count :]
    me = lax.axis_index(axis)
    halves = [lax.rem(me // (1 << b), 2) for b in bits]
    partners = [me + (1 - 2 * h) * (1 << b) for h, b in zip(halves, bits)]
    barrier = pltpu.get_barrier_semaphore()
    for p in partners:
        pl.semaphore_signal(barrier, inc=1, device_id={axis: p}, device_id_type=pl.DeviceIdType.MESH)
    pl.semaphore_wait(barrier, len(bits))

    starts = [[0] for _ in range(count)]
    for s in range(len(bits)):
        copies = []
        for i in range(count):
            size = inputs[i].shape[0] >> (s + 1)
            base = inputs[i].shape[0] - 2 * size
            source = inputs[i] if s == 0 else works[i]
            there = pl.multiple_of(starts[i][s] + (1 - halves[orders[i][s]]) * size, 8)
            copy = pltpu.make_async_remote_copy(
                src_ref=source.at[pl.ds(there, size)],
                dst_ref=recvs[i].at[pl.ds(base, size)],
                send_sem=send_sem.at[i, s],
                recv_sem=recv_sem.at[i, s],
                device_id={axis: partners[orders[i][s]]},
                device_id_type=pl.DeviceIdType.MESH,
            )
            copy.start()
            copies.append(copy)
        for i in range(count):
            size = inputs[i].shape[0] >> (s + 1)
            base = inputs[i].shape[0] - 2 * size
            source = inputs[i] if s == 0 else works[i]
            here = pl.multiple_of(starts[i][s] + halves[orders[i][s]] * size, 8)
            copies[i].wait()
            target = outs[i] if s == len(bits) - 1 else works[i]
            target[pl.ds(here, size), :] = source[pl.ds(here, size), :] + recvs[i][pl.ds(base, size), :]
            starts[i].append(here)
    for s in reversed(range(len(bits))):
        t = 2 * len(bits) - 1 - s
        copies = []
        for i in range(count):
            size = inputs[i].shape[0] >> (s + 1)
            mine = outs[i].at[pl.ds(starts[i][s + 1], size)]
            copy = pltpu.make_async_remote_copy(
                src_ref=mine,
                dst_ref=mine,
                send_sem=send_sem.at[i, t],
                recv_sem=recv_sem.at[i, t],
                device_id={axis: partners[orders[i][s]]},
                device_id_type=pl.DeviceIdType.MESH,
            )
            copy.start()
            copies.append(copy)
        for copy in copies:
            copy.wait()


def all_reduce(arrays, axis, size, collective_id):
    bits = list(range(size.bit_length() - 1))
    count = len(arrays)
    orders = [bits[t:] + bits[:t] for t in (min(1, max(0, i - 1)) for i in range(count))]
    total = sum(a.size for a in arrays)
    vmem = pl.BlockSpec(memory_space=pltpu.VMEM)
    return pl.pallas_call(
        functools.partial(reduce_kernel, axis, orders, count),
        out_shape=[jax.ShapeDtypeStruct(a.shape, a.dtype) for a in arrays],
        in_specs=[vmem] * count,
        out_specs=[vmem] * count,
        scratch_shapes=[pltpu.VMEM(a.shape, a.dtype) for a in arrays * 2]
        + [pltpu.SemaphoreType.DMA((count, 2 * len(bits))), pltpu.SemaphoreType.DMA((count, 2 * len(bits)))],
        compiler_params=pltpu.CompilerParams(
            collective_id=collective_id, has_side_effects=True, vmem_limit_bytes=16 * 2**20
        ),
        cost_estimate=pl.CostEstimate(flops=total, bytes_accessed=40 * total, transcendentals=0),
    )(*arrays)


def shards(row_size, col_size, momentum, grads, basis):
    rank = basis.shape[1]
    factor = (momentum.shape[0] * row_size * momentum.shape[1] * col_size / rank) ** 0.5
    eye = jnp.eye(rank, dtype=jnp.float32)
    state = momentum
    right = basis
    scale = None
    squares = None
    left = None
    change = 0.0
    steps = grads.shape[0]
    for step in range(steps):
        buffer = state + grads[step].astype(jnp.float32)
        partial_value = matmul(buffer, right, ((1,), (0,)), HIGH)
        if step == 0:
            (projected,) = all_reduce([partial_value], "col", col_size, 0)
        else:
            projected, squares = all_reduce([partial_value, squares], "col", col_size, 1)
            scale = lax.rsqrt(squares[:1] + norm_eps)
            projected = projected * scale
            change = change + factor * matmul(left, right * scale, ((1,), (1,)), HIGH)
        local = matmul(buffer, projected, ((0,), (0,)), HIGH)
        eighth = local.shape[0] // 8
        product = lax.psum(local[: 6 * eighth], "row")
        part = matmul(projected, projected, ((0,), (0,)), HIGHEST)
        gram, sixth, seventh = all_reduce(
            [part, local[6 * eighth : 7 * eighth], local[7 * eighth :]], "row", row_size, 2
        )
        product = jnp.concatenate([product, sixth, seventh])
        lower = jnp.linalg.cholesky(gram)
        inverse = jax.scipy.linalg.solve_triangular(lower, eye, lower=True)
        ortho = matmul(projected, inverse, ((1,), (1,)), HIGHEST)
        raw = matmul(product, inverse, ((1,), (1,)), HIGH)
        left = ortho
        squares = jnp.pad(jnp.sum(raw * raw, axis=0, keepdims=True), ((0, 8 * col_size - 1), (0, 0)))
        right = raw
        state = buffer - (1.0 - keep_rate) * matmul(
            ortho.astype(jnp.bfloat16), raw.astype(jnp.bfloat16), ((1,), (1,)), None
        )
    (squares,) = all_reduce([squares], "col", col_size, 3)
    scale = lax.rsqrt(squares[:1] + norm_eps)
    change = change + factor * matmul(left, right * scale, ((1,), (1,)), HIGH)
    return (change.astype(jnp.bfloat16), state)


def solution(mesh):
    return jax.shard_map(
        functools.partial(shards, mesh.shape["row"], mesh.shape["col"]),
        mesh=mesh,
        in_specs=(P("row", "col"), P(None, "row", "col"), P("col", None)),
        out_specs=(P("row", "col"), P("row", "col")),
        check_vma=False,
    )
```
